256 devices in a mesh: grp: 8 (over x_hi, y), row: 4 (over x_lo, core), col: 8 (over z).
Axes of the slice: x: 4 (x_hi: 2, x_lo: 2; x = x_hi * 2 + x_lo), y: 4, z: 8, core: 2. Of those that a mesh axis runs over, the one named last changes fastest.
Arguments:
- queries: bfloat16 [8192, 2560], P(('grp', 'col'), 'row'), may hold values from -70 to 70
- suffix_keys: bfloat16 [8192, 512], P(('grp', 'col'), 'row'), may hold values from -15 to 15
- suffix_values: bfloat16 [8192, 512], P(('grp', 'col'), 'row'), may hold values from -6 to 6
- prefix_keys: bfloat16 [8, 4096, 512], P('grp', 'col', 'row'), may hold values from -15 to 15
- prefix_values: bfloat16 [8, 4096, 512], P('grp', 'col', 'row'), may hold values from -6 to 6
- sink_logits: float32 [20], P('row'), may hold values from 0 to 14
- suffix_lengths: int32 [8, 4], P('grp'), may hold values from 1 to 512, 1024 in all within a row
- out_weight: bfloat16 [2560, 2560], P('row', 'col'), may hold values from -0.125 to 0.125
- residual: bfloat16 [8192, 2560], P(('grp', 'col'), 'row'), may hold values from -12 to 12
- norm_gain: float32 [2560], replicated, may hold values from 0.25 to 1.75
- expert_ids: int32 [8192, 6], P(('grp', 'col')), may hold values from 0 to 63, all different within a row; in each aligned block of 128 rows (0 to 127, 128 to 255, ...) at most 24 rows name the same one
- gate_fixed: int32 [8192, 6], P(('grp', 'col')), may hold values from 1 to 4095
- gate_weight: bfloat16 [64, 2560, 1536], P(('grp', 'col'), None, 'row'), may hold values from -0.125 to 0.125
- up_weight: bfloat16 [64, 2560, 1536], P(('grp', 'col'), None, 'row'), may hold values from -0.125 to 0.125
- down_weight: bfloat16 [64, 2560, 1536], P(('grp', 'col'), None, 'row'), may hold values from -0.15625 to 0.15625
Outputs:
- hidden_state: bfloat16 [8192, 2560], P(('grp', 'col'), 'row')
- expert_mix: bfloat16 [8192, 2560], P(('grp', 'col'), 'row')
The draws below stay inside these ranges and needn't reach their ends.
Inputs may be any that keep to these rules, and one draw needn't show every extreme that they name: `suffix_lengths`: each row holds the suffix lengths of one group's 4 requests and sums to 1024; the largest of each row is 512. `expert_ids`: each token names 6 different experts. In each aligned block of 128 rows no expert is named by more than 24 rows, a bound that some block reaches.
All inputs are finite; a program needn't handle non-finite values.
Results may differ from the reference program's by a relative error of at most 0.014.
Values may be sent and summed in bfloat16 or wider, within the bound.
No kernel may reach another device: no remote copies, remote signals or barrier semaphores. Data moves between devices by JAX's collectives and lax.ppermute only.
A program may use at most 128 MiB of HBM per device.

```python
import math
import jax
import jax.numpy as jnp
import numpy as np
from jax import lax

D = 2560
HEADS = 20
KVH = 4
HD = 128
FF = 1536
TOPK = 6
TOK = 128
PREFIX = 4096
REQ = 4
EXPERTS = 64
GROUPS = 8
SUFFIX = 1024
TOKENS = 8192
MAXLEN = 512
CAP = 24


def prefix_key_table(key):
    base = jnp.clip(jax.random.normal(jax.random.fold_in(key, 11), (GROUPS, PREFIX, KVH * HD), jnp.float32), -6.0, 6.0) * 2.5
    return base


def draw_prefix_keys(key, part):
    return prefix_key_table(key).astype(jnp.bfloat16)


def draw_sink_logits(key, part):
    centre = 3.1 + math.log(PREFIX + MAXLEN // 2)
    spread = jax.random.uniform(jax.random.fold_in(key, 41), (HEADS,), jnp.float32, -2.0, 1.0)
    return (centre + spread).astype(jnp.float32)


def draw_queries(key, part):
    base = jnp.clip(jax.random.normal(jax.random.fold_in(key, 23), (TOKENS, HEADS * HD), jnp.float32), -6.0, 6.0)
    return base.astype(jnp.bfloat16)


def draw_residual(key, part):
    key_base = jax.random.fold_in(key, 31)
    key_rows = jax.random.fold_in(key, 32)
    key_cols = jax.random.fold_in(key, 33)
    row_scale = jnp.exp(jax.random.uniform(key_rows, (TOKENS, 1), jnp.float32, math.log(0.1), math.log(1.0)))
    col_scale = jnp.exp(jax.random.uniform(key_cols, (1, D), jnp.float32, math.log(0.2), math.log(2.0)))
    base = jnp.clip(jax.random.normal(key_base, (TOKENS, D), jnp.float32), -6.0, 6.0)
    values = base * row_scale * col_scale
    return values.astype(jnp.bfloat16)


def touch_ends(array, rng, low, top_value):
    index_at = [jax.random.randint(jax.random.fold_in(rng, axis), (), 0, length) for axis, length in enumerate(array.shape)]
    main_axis = array.shape.index(max(array.shape))
    neighbour = index_at[:main_axis] + [(index_at[main_axis] + 1) % array.shape[main_axis]] + index_at[main_axis + 1:]
    return array.at[tuple(index_at)].set(low).at[tuple(neighbour)].set(top_value)


def levels(stream_key, dims, cuts, low, high):
    def one(dim, blocks):
        steps = jax.random.uniform(jax.random.fold_in(jax.random.fold_in(stream_key, 6), dim), (blocks,), jnp.float32, low / len(cuts), high / len(cuts))
        return jnp.repeat(jnp.exp(steps), dims[dim] // blocks).reshape((-1,) + (1,) * (len(dims) - dim - 1))

    level = one(*cuts[0])
    for cut in cuts[1:]:
        level = level * one(*cut)
    return level


def split_up(number_of, total, reach, skew):
    loads = [(1 << 20) // math.isqrt(grade ** skew) + 1 for grade in range(2, number_of + 1)]
    rest, given = total - reach - (number_of - 1), [1] * (number_of - 1)
    while rest > 0:
        candidates = [i for i in range(number_of - 1) if given[i] < reach]
        whole, left = sum([loads[i] for i in candidates]), rest
        for i in candidates:
            extra = min(reach - given[i], max(1, left * loads[i] // whole), rest)
            given[i] = given[i] + extra
            rest = rest - extra
    return np.array([reach] + given)


def uneven_parts(rng, number_of, total, limit, skew):
    if number_of == 2:
        one = jax.random.randint(rng, (), max(1, total - limit), min(limit, total - 1) + 1)
        return jnp.stack([one, total - one])
    sizes = jnp.asarray(split_up(number_of, total, limit, skew), jnp.int32)
    twos = (number_of - 1) // 2
    source_of, taker = sizes[1:1 + 2 * twos:2], sizes[2:2 + 2 * twos:2]
    margin = jnp.minimum(source_of - 1, limit - taker)
    passed = jax.random.randint(jax.random.fold_in(rng, 1), (twos,), 0, 1 << 20) % (margin + 1)
    sizes = sizes.at[1:1 + 2 * twos:2].set(source_of - passed).at[2:2 + 2 * twos:2].set(taker + passed)
    return sizes[jax.random.permutation(jax.random.fold_in(rng, 2), number_of)]


def shared_out(rng, own, number, rows, count, top, most, skew):
    order = jax.random.permutation(rng, count)
    crowded, ordinary = load_shares(count, rows * top, most, skew, True), load_shares(count, rows * top, most, skew, False)
    places = jnp.arange(count)

    def named(tallies, rotation):
        used = int((tallies > 0).sum())
        fixed = max(1, used // 4)
        moved = fixed + (places - fixed + rotation * (used - fixed)) % max(1, count - fixed)
        return jnp.zeros((count,), jnp.int32).at[order[jnp.where(places < fixed, places, moved)]].set(jnp.asarray(tallies, jnp.int32))

    tallies = jnp.where(number % 4 == 0, named(crowded, number // 4), named(ordinary, number - number // 4 - 1))
    mixed = jax.random.permutation(jax.random.fold_in(own, 3), count)
    source_of, sink = mixed[0:count // 2 * 2:2], mixed[1:count // 2 * 2:2]
    slack = jnp.minimum(tallies[source_of] - 1, most - tallies[sink]) // 2
    slack = jnp.where((source_of == order[0]) | (sink == order[0]) | (tallies[sink] == 0), 0, jnp.maximum(slack, 0))
    moved = jax.random.randint(jax.random.fold_in(own, 4), (count // 2,), 0, 1 << 20) % (slack + 1)
    tallies = tallies.at[source_of].add(-moved).at[sink].add(moved)
    items = jnp.searchsorted(jnp.cumsum(tallies), jnp.arange(rows * top), side="right").astype(jnp.int32)
    table = items.reshape(top, rows).T
    table = table[jax.random.permutation(jax.random.fold_in(own, 1), rows)]
    rotation = jax.random.randint(jax.random.fold_in(own, 2), (rows, 1), 0, top)
    return jnp.take_along_axis(table, (jnp.arange(top)[None, :] + rotation) % top, axis=1)


def load_shares(amount, total, most, lean, full):
    portions = [(1 << 20) // math.isqrt(rank ** lean) + 1 for rank in range(1, amount + 1)]
    largest = most if full else min(most, max(-(-total // amount), total * portions[0] // sum(portions)))
    least = 1 if total - largest >= amount - 1 else 0
    holding, spare = [largest] + [least] * (amount - 1), total - largest - least * (amount - 1)
    while spare > 0:
        movable = [i for i in range(1, amount) if holding[i] < largest] or [i for i in range(1, amount) if holding[i] < most]
        mass, left = sum([portions[i] for i in movable]), spare
        for i in movable:
            extra = min(most - holding[i], max(1, left * portions[i] // mass), spare)
            holding[i] = holding[i] + extra
            spare = spare - extra
    return np.array(holding)


def noise(stream_key, dims, scale, limit, split=(), kind=jnp.bfloat16):
    drawn = scale * jax.random.normal(stream_key, dims, jnp.float32)
    if split:
        drawn = drawn * levels(stream_key, dims, split, -0.22, 0.18)
    return jnp.clip(drawn, -limit, limit).astype(kind)


def setup_inputs(seed: int = 0) -> dict:
    keys = jax.random.split(jax.random.key(seed), 16)
    queries = draw_queries(jax.random.fold_in(keys[15], 71), 0)
    suffix_keys = noise(keys[1], (TOKENS, KVH * HD), 2.5, 15.0, ((0, 64), (1, 4)))
    suffix_values = noise(keys[2], (TOKENS, KVH * HD), 1.0, 6.0, ((0, 64), (1, 4)))
    prefix_keys = draw_prefix_keys(jax.random.fold_in(keys[15], 71), 0)
    prefix_values = noise(keys[4], (GROUPS, PREFIX, KVH * HD), 1.0, 6.0, ((0, 8), (1, 8), (2, 4)))
    sink_logits = draw_sink_logits(jax.random.fold_in(keys[15], 71), 0)
    suffix_lengths = jax.vmap(lambda own: uneven_parts(own, REQ, SUFFIX, MAXLEN, 2))(jax.random.split(keys[6], GROUPS)).reshape((GROUPS, REQ)).astype(jnp.int32)
    out_weight = noise(keys[7], (HEADS * HD, D), (HEADS * HD) ** -0.5, 0.125, ((0, 4), (1, 8)))
    residual = draw_residual(jax.random.fold_in(keys[15], 71), 0)
    norm_gain = jnp.clip(1.0 + 0.15 * jax.random.normal(keys[9], (D,), jnp.float32), 0.25, 1.75)
    expert_ids_keys = jax.random.split(jax.random.fold_in(keys[10], 1), TOKENS // TOK)
    expert_ids_turns = jax.random.permutation(jax.random.fold_in(keys[10], 3), TOKENS // TOK)
    expert_ids = jax.vmap(lambda own, number: shared_out(jax.random.fold_in(keys[10], 2), own, number, TOK, EXPERTS, TOPK, CAP, 2))(expert_ids_keys, expert_ids_turns).reshape((TOKENS, TOPK))
    gate_fixed = touch_ends(jax.random.randint(keys[11], (TOKENS, TOPK), 1, 4096), jax.random.fold_in(keys[11], 1), 1, 4095).astype(jnp.int32)
    gate_weight = noise(keys[12], (EXPERTS, D, FF), D ** -0.5, 0.125, ((0, 64), (2, 4)))
    up_weight = noise(keys[13], (EXPERTS, D, FF), D ** -0.5, 0.125, ((0, 64), (2, 4)))
    down_weight = noise(keys[14], (EXPERTS, D, FF), FF ** -0.5, 0.15625, ((0, 64), (2, 4)))
    return {"queries": queries, "suffix_keys": suffix_keys, "suffix_values": suffix_values, "prefix_keys": prefix_keys, "prefix_values": prefix_values, "sink_logits": sink_logits, "suffix_lengths": suffix_lengths, "out_weight": out_weight, "residual": residual, "norm_gain": norm_gain, "expert_ids": expert_ids, "gate_fixed": gate_fixed, "gate_weight": gate_weight, "up_weight": up_weight, "down_weight": down_weight}


eps = 1e-06

def segment_of(positions, lengths):
    ends = jnp.cumsum(lengths).astype(jnp.int32)
    return lax.optimization_barrier(jnp.sum((positions[:, None] >= ends[None, :]).astype(jnp.int32), axis=1))

def normalize(rows, gain):
    values = rows.astype(jnp.float32)
    mean_square = lax.optimization_barrier(jnp.mean(values * values, axis=-1, keepdims=True))
    return (values * lax.rsqrt(mean_square + eps) * gain).astype(jnp.bfloat16)

def group_attention(operands):
    group_queries, keys_suffix, values_suffix, keys_prefix, values_prefix, lengths, sinks = operands
    group_size = HEADS // KVH
    positions = jnp.arange(SUFFIX, dtype=jnp.int32)
    segments = segment_of(positions, lengths)
    visible = (segments[:, None] == segments[None, :]) & (positions[None, :] <= positions[:, None])
    visible = jnp.concatenate([jnp.ones((SUFFIX, PREFIX), dtype=bool), visible], axis=1)
    keys_all = jnp.concatenate([keys_prefix, keys_suffix], axis=0).astype(jnp.float32).reshape(PREFIX + SUFFIX, KVH, HD)
    values_all = jnp.concatenate([values_prefix, values_suffix], axis=0).astype(jnp.float32).reshape(PREFIX + SUFFIX, KVH, HD)
    query_blocks = group_queries.astype(jnp.float32).reshape(SUFFIX, KVH, group_size, HD)
    sink_heads = sinks.reshape(KVH, group_size)

    def per_head(args):
        query_group, key_head, value_head, sink_group = args
        scores = jnp.einsum('sgd,pd->gsp', query_group, key_head) * HD ** (-0.5)
        scores = jnp.where(visible[None], scores, -1e+30)
        row_max = jnp.maximum(lax.optimization_barrier(jnp.max(scores, axis=-1)), sink_group[:, None])
        weights = jnp.where(visible[None], jnp.exp(scores - row_max[..., None]), 0.0)
        norm_total = lax.optimization_barrier(jnp.sum(weights, axis=-1)) + jnp.exp(sink_group[:, None] - row_max)
        probs = lax.optimization_barrier(weights.astype(jnp.bfloat16)).astype(jnp.float32)
        mixed = jnp.einsum('gsp,pd->gsd', probs, value_head)
        return mixed / norm_total[..., None]
    heads_out = lax.map(per_head, (query_blocks.transpose(1, 0, 2, 3), keys_all.transpose(1, 0, 2), values_all.transpose(1, 0, 2), sink_heads))
    return heads_out.transpose(2, 0, 1, 3).reshape(SUFFIX, HEADS * HD).astype(jnp.bfloat16)

def reference(queries, suffix_keys, suffix_values, prefix_keys, prefix_values, sink_logits, suffix_lengths, out_weight, residual, norm_gain, expert_ids, gate_fixed, gate_weight, up_weight, down_weight):
    sinks_all = jnp.broadcast_to(sink_logits[None, :], (GROUPS, HEADS))
    attended = lax.map(group_attention, (queries.reshape(GROUPS, SUFFIX, HEADS * HD), suffix_keys.reshape(GROUPS, SUFFIX, KVH * HD), suffix_values.reshape(GROUPS, SUFFIX, KVH * HD), prefix_keys, prefix_values, suffix_lengths, sinks_all))
    attended = attended.reshape(TOKENS, HEADS * HD)
    projected = jnp.dot(attended, out_weight, preferred_element_type=jnp.float32)
    hidden_state = (residual.astype(jnp.float32) + projected).astype(jnp.bfloat16)
    normed = normalize(hidden_state, norm_gain)
    shares = gate_fixed.astype(jnp.float32)
    shares = shares / lax.optimization_barrier(jnp.sum(shares, axis=1, keepdims=True))
    flat_experts = expert_ids.reshape(-1).astype(jnp.int32)
    padded_rows = jnp.concatenate([normed, jnp.zeros((1, D), jnp.bfloat16)], axis=0)
    flat_shares = jnp.concatenate([shares.reshape(-1), jnp.zeros((1,), jnp.float32)], axis=0)

    def per_expert(carry, operands):
        expert, gate_w, up_w, down_w = operands
        picks = jnp.nonzero(flat_experts == expert, size=EXPERTS * CAP, fill_value=TOKENS * TOPK)[0].astype(jnp.int32)
        owners = (picks // TOPK).astype(jnp.int32)
        rows = padded_rows[owners]
        gate = jnp.dot(rows, gate_w, preferred_element_type=jnp.float32)
        upper = jnp.dot(rows, up_w, preferred_element_type=jnp.float32)
        active = (jax.nn.silu(gate) * upper).astype(jnp.bfloat16)
        out_rows = lax.dot_general(active, down_w, (((1,), (1,)), ((), ())), preferred_element_type=jnp.float32)
        out_rows = lax.optimization_barrier(out_rows.astype(jnp.bfloat16)).astype(jnp.float32)
        carry = carry.at[owners].add(flat_shares[picks][:, None] * out_rows)
        return (carry, None)
    mixed, unused = lax.scan(per_expert, jnp.zeros((TOKENS + 1, D), jnp.float32), (jnp.arange(EXPERTS, dtype=jnp.int32), gate_weight, up_weight, down_weight))
    expert_mix = mixed[:TOKENS].astype(jnp.bfloat16)
    return (hidden_state, expert_mix)
```

```python
import functools

import jax
import jax.numpy as jnp
from jax import lax
from jax.experimental import pallas as pl
from jax.experimental.pallas import tpu as pltpu
from jax.sharding import PartitionSpec as P

HD = 128
TOPK = 6
CAP = 24
CHUNKS = 1
PAD = 16
eps = 1e-06
BF = jnp.bfloat16
F32 = jnp.float32
VMEM = pl.BlockSpec(memory_space=pltpu.VMEM)
SMEM = pl.BlockSpec(memory_space=pltpu.SMEM)
PARAMS = pltpu.CompilerParams(vmem_limit_bytes=56 * 1024 * 1024)


def matmul_t(a, b):
    return lax.dot_general(a, b, (((1,), (1,)), ((), ())), preferred_element_type=F32)


def attend_kernel(first, last, offsets, ring, info_ref, sink_ref, q_ref, *refs):
    split = last
    count = 2 if split else len(offsets)
    blocks, refs = refs[:count], refs[count:]
    tokens = q_ref.shape[0]
    heads = q_ref.shape[1] // HD
    rows = tokens * heads
    q = jnp.concatenate([q_ref[:, h * HD : (h + 1) * HD] for h in range(heads)], axis=0)
    if first:
        top = jnp.concatenate(
            [jnp.full((tokens, 1), sink_ref[h], F32) for h in range(heads)], axis=0
        )
        total = jnp.ones((rows, 1), F32)
        acc = jnp.zeros((rows, HD), F32)
    else:
        top, total, acc = refs[0][:, :1], refs[1][:, :1], refs[2][...]
        refs = refs[3:]
    z = info_ref[4]
    token = lax.rem(lax.broadcasted_iota(jnp.int32, (rows, 1), 0), tokens)
    q_pos = z * tokens + token
    begin = jnp.zeros_like(q_pos)
    for i in range(4):
        end = info_ref[i]
        begin = jnp.maximum(begin, jnp.where(q_pos >= end, end, 0))
    for i, offset in enumerate(offsets):
        if split:
            keys, values = blocks[0][...], blocks[1][...]
        else:
            half = blocks[i].shape[0] // 2
            keys, values = blocks[i][:half], blocks[i][half:]
        shared = keys.shape[0] - tokens
        scores = matmul_t(q, keys) * HD ** (-0.5)
        source = lax.rem(z - offset + ring, ring)
        k_pos = source * tokens + lax.broadcasted_iota(jnp.int32, (1, tokens), 1)
        visible = (k_pos >= begin) & (k_pos <= q_pos)
        scores = jnp.concatenate(
            [scores[:, :shared], jnp.where(visible, scores[:, shared:], -1e30)], axis=1
        )
        new_top = jnp.maximum(top, jnp.max(scores, axis=1, keepdims=True))
        weights = jnp.exp(scores - new_top)
        factor = jnp.exp(top - new_top)
        total = total * factor + jnp.sum(weights, axis=1, keepdims=True)
        acc = acc * factor + jnp.dot(weights.astype(BF), values, preferred_element_type=F32)
        top = new_top
    if last:
        out = (acc / total).astype(BF)
        for h in range(heads):
            refs[0][:, h * HD : (h + 1) * HD] = out[h * tokens : (h + 1) * tokens]
    else:
        refs[0][...] = jnp.broadcast_to(top, (rows, HD))
        refs[1][...] = jnp.broadcast_to(total, (rows, HD))
        refs[2][...] = acc


def attend(info, sinks, queries, state, blocks, offsets, ring, last):
    tokens = queries.shape[0]
    rows = tokens * (queries.shape[1] // HD)
    first = state is None
    state = () if first else tuple(state)
    if last:
        out_shape = jax.ShapeDtypeStruct(queries.shape, BF)
        out_specs = VMEM
    else:
        out_shape = (jax.ShapeDtypeStruct((rows, HD), F32),) * 3
        out_specs = (VMEM,) * 3
    return pl.pallas_call(
        functools.partial(attend_kernel, first, last, tuple(offsets), ring),
        out_shape=out_shape,
        in_specs=[SMEM, SMEM] + [VMEM] * (1 + len(blocks) + len(state)),
        out_specs=out_specs,
        compiler_params=PARAMS,
        name="attend",
    )(info, sinks, queries, *blocks, *state)


def project_kernel(stride, r_ref, a_ref, w_ref, own_ref, across_ref, pair_ref):
    r = r_ref[0]
    width = own_ref.shape[1] // 2
    a = a_ref[...]
    for j in range(4):
        for half in range(2):
            block = (r ^ j) * 2 + half
            w = w_ref[pl.ds(pl.multiple_of(block * stride, 16), width), :]
            part = matmul_t(a, w)
            cols = slice(half * width, (half + 1) * width)
            if j == 0:
                own_ref[:, cols] = part
            elif j == 2:
                across_ref[:, cols] = part
            else:
                pair_ref[j // 2, :, cols] = part.astype(BF)


def project(r, attended, gathered, stride):
    tokens = attended.shape[0]
    width = 2 * (stride - PAD)
    return pl.pallas_call(
        functools.partial(project_kernel, stride),
        out_shape=(
            jax.ShapeDtypeStruct((tokens, width), F32),
            jax.ShapeDtypeStruct((tokens, width), F32),
            jax.ShapeDtypeStruct((2, tokens, width), BF),
        ),
        in_specs=[SMEM, VMEM, VMEM],
        out_specs=(VMEM, VMEM, VMEM),
        compiler_params=PARAMS,
        name="project",
    )(r, attended, gathered)


def routing(ids, z, ring):
    tokens = ids.shape[1]
    experts = (lax.broadcasted_iota(jnp.int32, (8, tokens), 0) * ring + z).astype(F32)
    hits = [(ids[k : k + 1] == experts).astype(F32) for k in range(TOPK)]
    chosen = sum(hits)
    before = (
        lax.broadcasted_iota(jnp.int32, (tokens, tokens), 0)
        < lax.broadcasted_iota(jnp.int32, (tokens, tokens), 1)
    ).astype(BF)
    slot = jnp.dot(chosen.astype(BF), before, preferred_element_type=F32)
    slot = jnp.where(chosen > 0, slot, -1.0)
    place = lax.broadcasted_iota(jnp.int32, (8, CAP, tokens), 1).astype(F32)
    picks = (place == slot[:, None, :]).astype(F32)
    return hits, picks


def table_of(ex_ref, source):
    return ex_ref[source, :, :].astype(F32)


def select_kernel(offsets, ring, z_ref, ex_ref, *refs):
    z = z_ref[0]
    out_ref = refs[-1]
    for i, offset in enumerate(offsets):
        table = table_of(ex_ref, lax.rem(z - offset + ring, ring))
        tokens = refs[i].shape[0]
        _, picks = routing(table[:TOPK, :tokens], z, ring)
        picks = picks.reshape(8 * CAP, tokens).astype(BF)
        rows = jnp.dot(picks, refs[i][...], preferred_element_type=F32).astype(BF)
        for g in range(8):
            out_ref[g, i * CAP : (i + 1) * CAP, :] = rows[g * CAP : (g + 1) * CAP]


def select(z, extras, blocks, offsets, ring):
    width = blocks[0].shape[1]
    return pl.pallas_call(
        functools.partial(select_kernel, tuple(offsets), ring),
        out_shape=jax.ShapeDtypeStruct((8, CAP * len(blocks), width), BF),
        in_specs=[SMEM, VMEM] + [VMEM] * len(blocks),
        out_specs=VMEM,
        compiler_params=PARAMS,
        name="select",
    )(z, extras, *blocks)


def combine_kernel(offsets, ring, z_ref, ex_ref, ret_ref, out_ref):
    z = z_ref[0]
    tokens = out_ref.shape[1]
    for i, offset in enumerate(offsets):
        table = table_of(ex_ref, lax.rem(z - offset + ring, ring))
        hits, picks = routing(table[:TOPK, :tokens], z, ring)
        gates = 64.0 * table[:TOPK, tokens : 2 * tokens] + table[:TOPK, 2 * tokens : 3 * tokens]
        shares = gates / jnp.sum(gates, axis=0, keepdims=True)
        mine = sum(hits[k] * shares[k : k + 1] for k in range(TOPK))
        weights = (picks * mine[:, None, :]).reshape(8 * CAP, tokens)
        high = weights.astype(BF)
        low = (weights - high.astype(F32)).astype(BF)
        rows = jnp.concatenate([ret_ref[g, i * CAP : (i + 1) * CAP, :] for g in range(8)], axis=0)
        dims = (((0,), (0,)), ((), ()))
        out_ref[i] = lax.dot_general(
            high, rows, dims, preferred_element_type=F32
        ) + lax.dot_general(low, rows, dims, preferred_element_type=F32)


def combine(z, extras, returned, offsets, ring, tokens):
    width = returned.shape[2]
    return pl.pallas_call(
        functools.partial(combine_kernel, tuple(offsets), ring),
        out_shape=jax.ShapeDtypeStruct((len(offsets), tokens, width), F32),
        in_specs=[SMEM, VMEM, VMEM],
        out_specs=VMEM,
        compiler_params=PARAMS,
        name="combine",
    )(z, extras, returned)


def ffn_kernel(r_ref, gain_ref, wg_ref, wu_ref, wd_ref, x0, x1, x2, x3, o0, o13, o2):
    r = r_ref[0]
    parts = [x[...].astype(F32) for x in (x0, x1, x2, x3)]
    width = parts[0].shape[1]
    square = sum(jnp.sum(p * p, axis=1, keepdims=True) for p in parts)
    scale = lax.rsqrt(square * (1.0 / (4 * width)) + eps)
    gate, upper = 0.0, 0.0
    for j in range(4):
        at = pl.ds(pl.multiple_of((r ^ j) * width, 128), width)
        normed = (parts[j] * scale * gain_ref[pl.ds(r ^ j, 1), :]).astype(BF)
        gate = gate + jnp.dot(normed, wg_ref[at, :], preferred_element_type=F32)
        upper = upper + jnp.dot(normed, wu_ref[at, :], preferred_element_type=F32)
    active = (gate / (1.0 + jnp.exp(-gate)) * upper).astype(BF)
    for j in range(4):
        at = pl.ds(pl.multiple_of((r ^ j) * width, 128), width)
        terms = matmul_t(active, wd_ref[at, :]).astype(BF)
        if j == 0:
            o0[...] = terms
        elif j == 2:
            o2[...] = terms
        else:
            o13[j // 2] = terms


def ffn(r, gain, wg, wu, wd, parts):
    rows, width = parts[0].shape
    step = 256 if rows % 256 == 0 else 192
    whole = pl.BlockSpec(wg.shape, lambda i: (0, 0))
    tile = pl.BlockSpec((step, width), lambda i: (i, 0))
    return pl.pallas_call(
        ffn_kernel,
        grid=(rows // step,),
        out_shape=(
            jax.ShapeDtypeStruct((rows, width), BF),
            jax.ShapeDtypeStruct((2, rows, width), BF),
            jax.ShapeDtypeStruct((rows, width), BF),
        ),
        in_specs=[SMEM, pl.BlockSpec(gain.shape, lambda i: (0, 0)), whole, whole, whole] + [tile] * 4,
        out_specs=(tile, pl.BlockSpec((2, step, width), lambda i: (0, i, 0)), tile),
        compiler_params=PARAMS,
        name="ffn",
    )(r, gain, wg, wu, wd, *parts)


def local(
    queries,
    suffix_keys,
    suffix_values,
    prefix_keys,
    prefix_values,
    sink_logits,
    suffix_lengths,
    out_weight,
    residual,
    norm_gain,
    expert_ids,
    gate_fixed,
    gate_weight,
    up_weight,
    down_weight,
):
    tokens = queries.shape[0]
    ring = lax.axis_size("col")
    rows4 = lax.axis_size("row")
    z = lax.axis_index("col").astype(jnp.int32)
    z1 = z.reshape(1)
    r1 = lax.axis_index("row").astype(jnp.int32).reshape(1)
    ends = jnp.cumsum(suffix_lengths[0]).astype(jnp.int32)
    info = jnp.concatenate([ends, z1])

    def shift(x, k):
        return lax.ppermute(x, "col", [(i, (i + k) % ring) for i in range(ring)])

    def swap(x, k):
        return lax.ppermute(x, "row", [(i, i ^ k) for i in range(rows4)])

    def both_ways(own, low, high):
        found = {0: own}
        up, down = own, own
        for k in range(1, 4):
            up, down = shift(up, 1), shift(down, -1)
            found[k], found[-k] = up, down
        found[4] = (shift(low(up), 1), shift(high(down), -1))
        return found

    half = prefix_keys.shape[1] + tokens
    kv = jnp.concatenate([prefix_keys[0], suffix_keys, prefix_values[0], suffix_values], axis=0)
    found = both_ways(kv, lambda x: x[:half], lambda x: x[half:])
    gates = gate_fixed.T
    table = jnp.concatenate([expert_ids.T, gates // 64, gates % 64], axis=1).astype(BF)
    columns, features = out_weight.shape[1], out_weight.shape[0]
    table = jnp.pad(table, ((0, PAD - TOPK), (0, features - table.shape[1])))
    gathered = lax.all_gather(
        jnp.concatenate([out_weight.T, table], axis=0), "col", axis=0, tiled=True
    )
    stride = columns + PAD
    extras = gathered.reshape(ring, stride, features)[:, columns:, : 3 * tokens]

    sinks = sink_logits
    state = attend(
        info, sinks, queries, None, [found[k] for k in (0, 1, -1)], (0, 1, -1), ring, False
    )
    for k in (2, 3):
        state = attend(
            info, sinks, queries, state, [found[k], found[-k]], (k, -k), ring, False
        )
    attended = attend(info, sinks, queries, state, found[4], (4,), ring, True)
    own, across, pair = project(r1, attended, gathered, stride)
    pair = swap(pair, 1).astype(F32)
    across = swap((across + pair[1]).astype(BF), 2).astype(F32)
    hidden = (residual.astype(F32) + (own + pair[0] + across)).astype(BF)

    middle = tokens // 2
    found = both_ways(hidden, lambda x: x[:middle], lambda x: x[middle:])
    found[4] = jnp.concatenate(found[4], axis=0)
    order = (0, 1, -1, 2, -2, 3, -3, 4)
    size = len(order) // CHUNKS
    gain = norm_gain.reshape(rows4, -1)
    width = hidden.shape[1]
    sums = {}
    for c in range(CHUNKS):
        offsets = order[c * size : (c + 1) * size]
        outgoing = select(z1, extras, [found[k] for k in offsets], offsets, ring)
        received = lax.all_to_all(outgoing, "grp", split_axis=0, concat_axis=0, tiled=True)
        x0 = received.reshape(-1, width)
        x2 = swap(x0, 2)
        x1 = swap(x0, 1)
        x3 = swap(x2, 1)
        o0, o13, o2 = ffn(r1, gain, gate_weight[0], up_weight[0], down_weight[0], (x0, x1, x2, x3))
        k13 = swap(o13, 1).astype(F32)
        far = swap((o2.astype(F32) + k13[1]).astype(BF), 2)
        result = (o0.astype(F32) + k13[0] + far.astype(F32)).astype(BF)
        returned = lax.all_to_all(
            result.reshape(outgoing.shape), "grp", split_axis=0, concat_axis=0, tiled=True
        )
        mixed = combine(z1, extras, returned, offsets, ring, tokens)
        for i, k in enumerate(offsets):
            sums[k] = mixed[i]

    low = shift(sums[4][:middle].astype(BF), -1).astype(F32)
    high = shift(sums[4][middle:].astype(BF), 1).astype(F32)
    down = sums[3] + jnp.pad(low, ((0, middle), (0, 0)))
    up = sums[-3] + jnp.pad(high, ((middle, 0), (0, 0)))
    for k in (2, 1, 0):
        down = shift(down.astype(BF), -1).astype(F32)
        up = shift(up.astype(BF), 1).astype(F32)
        if k:
            down = sums[k] + down
            up = sums[-k] + up
    expert_mix = (sums[0] + down + up).astype(BF)
    return (hidden, expert_mix)


def solution(mesh):
    placed = (
        P(("grp", "col"), "row"),
        P(("grp", "col"), "row"),
        P(("grp", "col"), "row"),
        P("grp", "col", "row"),
        P("grp", "col", "row"),
        P("row"),
        P("grp", None),
        P("row", "col"),
        P(("grp", "col"), "row"),
        P(),
        P(("grp", "col"), None),
        P(("grp", "col"), None),
        P(("grp", "col"), None, "row"),
        P(("grp", "col"), None, "row"),
        P(("grp", "col"), None, "row"),
    )
    return jax.shard_map(
        local,
        mesh=mesh,
        in_specs=placed,
        out_specs=(P(("grp", "col"), "row"), P(("grp", "col"), "row")),
        check_vma=False,
    )
```

```python
import functools

import jax
import jax.numpy as jnp
from jax import lax
from jax.experimental import pallas as pl
from jax.experimental.pallas import tpu as pltpu
from jax.sharding import PartitionSpec as P

HD = 128
TOPK = 6
CAP = 24
CHUNKS = 2
PAD = 16
eps = 1e-06
BF = jnp.bfloat16
F32 = jnp.float32
VMEM = pl.BlockSpec(memory_space=pltpu.VMEM)
SMEM = pl.BlockSpec(memory_space=pltpu.SMEM)
PARAMS = pltpu.CompilerParams(vmem_limit_bytes=56 * 1024 * 1024)


def matmul_t(a, b):
    return lax.dot_general(a, b, (((1,), (1,)), ((), ())), preferred_element_type=F32)


def attend_kernel(first, last, offsets, ring, info_ref, sink_ref, q_ref, *refs):
    count = 2 if last else len(offsets)
    blocks, refs = refs[:count], refs[count:]
    tokens = q_ref.shape[0]
    q = q_ref[...]
    if first:
        top = jnp.full((tokens, 1), sink_ref[pl.program_id(0)], F32)
        total = jnp.ones((tokens, 1), F32)
        acc = jnp.zeros((tokens, HD), F32)
    else:
        top, total, acc = refs[0][:, :1], refs[1][:, :1], refs[2][...]
        refs = refs[3:]
    z = info_ref[4]
    q_pos = z * tokens + lax.broadcasted_iota(jnp.int32, (tokens, 1), 0)
    begin = jnp.zeros_like(q_pos)
    for i in range(4):
        end = info_ref[i]
        begin = jnp.maximum(begin, jnp.where(q_pos >= end, end, 0))
    for i, offset in enumerate(offsets):
        if last:
            keys, values = blocks[0][...], blocks[1][...]
        else:
            half = blocks[i].shape[0] // 2
            keys, values = blocks[i][:half], blocks[i][half:]
        shared = keys.shape[0] - tokens
        scores = matmul_t(q, keys) * HD ** (-0.5)
        source = lax.rem(z - offset + ring, ring)
        k_pos = source * tokens + lax.broadcasted_iota(jnp.int32, (1, tokens), 1)
        visible = (k_pos >= begin) & (k_pos <= q_pos)
        scores = jnp.concatenate(
            [scores[:, :shared], jnp.where(visible, scores[:, shared:], -1e30)], axis=1
        )
        new_top = jnp.maximum(top, jnp.max(scores, axis=1, keepdims=True))
        weights = jnp.exp(scores - new_top)
        factor = jnp.exp(top - new_top)
        total = total * factor + jnp.sum(weights, axis=1, keepdims=True)
        acc = acc * factor + jnp.dot(weights.astype(BF), values, preferred_element_type=F32)
        top = new_top
    if last:
        refs[0][...] = (acc / total).astype(BF)
    else:
        refs[0][...] = jnp.broadcast_to(top, (tokens, HD))
        refs[1][...] = jnp.broadcast_to(total, (tokens, HD))
        refs[2][...] = acc


def attend(info, sinks, queries, state, blocks, offsets, ring, last):
    tokens = queries.shape[0]
    heads = queries.shape[1] // HD
    rows = tokens * heads
    first = state is None
    state = () if first else tuple(state)
    column = pl.BlockSpec((tokens, HD), lambda h: (0, h))
    band = pl.BlockSpec((tokens, HD), lambda h: (h, 0))
    if last:
        out_shape = jax.ShapeDtypeStruct(queries.shape, BF)
        out_specs = column
    else:
        out_shape = (jax.ShapeDtypeStruct((rows, HD), F32),) * 3
        out_specs = (band,) * 3
    return pl.pallas_call(
        functools.partial(attend_kernel, first, last, tuple(offsets), ring),
        grid=(heads,),
        out_shape=out_shape,
        in_specs=[SMEM, SMEM, column]
        + [pl.BlockSpec(x.shape, lambda h: (0, 0)) for x in blocks]
        + [band] * len(state),
        out_specs=out_specs,
        compiler_params=PARAMS,
        name="attend",
    )(info, sinks, queries, *blocks, *state)


def project_kernel(stride, r_ref, a_ref, w_ref, own_ref, across_ref, pair_ref):
    r = r_ref[0]
    width = own_ref.shape[1] // 2
    a = a_ref[...]
    for j in range(4):
        for half in range(2):
            block = (r ^ j) * 2 + half
            w = w_ref[pl.ds(pl.multiple_of(block * stride, 16), width), :]
            part = matmul_t(a, w)
            cols = slice(half * width, (half + 1) * width)
            if j == 0:
                own_ref[:, cols] = part
            elif j == 2:
                across_ref[:, cols] = part
            else:
                pair_ref[j // 2, :, cols] = part.astype(BF)


def project(r, attended, gathered, stride):
    tokens = attended.shape[0]
    width = 2 * (stride - PAD)
    return pl.pallas_call(
        functools.partial(project_kernel, stride),
        out_shape=(
            jax.ShapeDtypeStruct((tokens, width), F32),
            jax.ShapeDtypeStruct((tokens, width), F32),
            jax.ShapeDtypeStruct((2, tokens, width), BF),
        ),
        in_specs=[SMEM, VMEM, VMEM],
        out_specs=(VMEM, VMEM, VMEM),
        compiler_params=PARAMS,
        name="project",
    )(r, attended, gathered)


def routing(ids, z, ring):
    tokens = ids.shape[1]
    experts = (lax.broadcasted_iota(jnp.int32, (8, tokens), 0) * ring + z).astype(F32)
    hits = [(ids[k : k + 1] == experts).astype(F32) for k in range(TOPK)]
    chosen = sum(hits)
    before = (
        lax.broadcasted_iota(jnp.int32, (tokens, tokens), 0)
        < lax.broadcasted_iota(jnp.int32, (tokens, tokens), 1)
    ).astype(BF)
    slot = jnp.dot(chosen.astype(BF), before, preferred_element_type=F32)
    slot = jnp.where(chosen > 0, slot, -1.0)
    place = lax.broadcasted_iota(jnp.int32, (8, CAP, tokens), 1).astype(F32)
    picks = (place == slot[:, None, :]).astype(F32)
    return hits, picks


def table_of(ex_ref, source):
    return ex_ref[source, :, :].astype(F32)


def select_kernel(offsets, ring, z_ref, ex_ref, *refs):
    z = z_ref[0]
    out_ref = refs[-1]
    for i, offset in enumerate(offsets):
        table = table_of(ex_ref, lax.rem(z - offset + ring, ring))
        tokens = refs[i].shape[0]
        _, picks = routing(table[:TOPK, :tokens], z, ring)
        picks = picks.reshape(8 * CAP, tokens).astype(BF)
        rows = jnp.dot(picks, refs[i][...], preferred_element_type=F32).astype(BF)
        for g in range(8):
            out_ref[g, i * CAP : (i + 1) * CAP, :] = rows[g * CAP : (g + 1) * CAP]


def select(z, extras, blocks, offsets, ring):
    width = blocks[0].shape[1]
    return pl.pallas_call(
        functools.partial(select_kernel, tuple(offsets), ring),
        out_shape=jax.ShapeDtypeStruct((8, CAP * len(blocks), width), BF),
        in_specs=[SMEM, VMEM] + [VMEM] * len(blocks),
        out_specs=VMEM,
        compiler_params=PARAMS,
        name="select",
    )(z, extras, *blocks)


def combine_kernel(offsets, ring, z_ref, ex_ref, ret_ref, out_ref):
    z = z_ref[0]
    tokens = out_ref.shape[1]
    for i, offset in enumerate(offsets):
        table = table_of(ex_ref, lax.rem(z - offset + ring, ring))
        hits, picks = routing(table[:TOPK, :tokens], z, ring)
        gates = 64.0 * table[:TOPK, tokens : 2 * tokens] + table[:TOPK, 2 * tokens : 3 * tokens]
        shares = gates / jnp.sum(gates, axis=0, keepdims=True)
        mine = sum(hits[k] * shares[k : k + 1] for k in range(TOPK))
        weights = (picks * mine[:, None, :]).reshape(8 * CAP, tokens)
        high = weights.astype(BF)
        low = (weights - high.astype(F32)).astype(BF)
        rows = jnp.concatenate([ret_ref[g, i * CAP : (i + 1) * CAP, :] for g in range(8)], axis=0)
        dims = (((0,), (0,)), ((), ()))
        out_ref[i] = lax.dot_general(
            high, rows, dims, preferred_element_type=F32
        ) + lax.dot_general(low, rows, dims, preferred_element_type=F32)


def combine(z, extras, returned, offsets, ring, tokens):
    width = returned.shape[2]
    return pl.pallas_call(
        functools.partial(combine_kernel, tuple(offsets), ring),
        out_shape=jax.ShapeDtypeStruct((len(offsets), tokens, width), F32),
        in_specs=[SMEM, VMEM, VMEM],
        out_specs=VMEM,
        compiler_params=PARAMS,
        name="combine",
    )(z, extras, returned)


def ffn_kernel(r_ref, gain_ref, wg_ref, wu_ref, wd_ref, x0, x1, x2, x3, o0, o13, o2):
    r = r_ref[0]
    parts = [x[...].astype(F32) for x in (x0, x1, x2, x3)]
    width = parts[0].shape[1]
    square = sum(jnp.sum(p * p, axis=1, keepdims=True) for p in parts)
    scale = lax.rsqrt(square * (1.0 / (4 * width)) + eps)
    gate, upper = 0.0, 0.0
    for j in range(4):
        at = pl.ds(pl.multiple_of((r ^ j) * width, 128), width)
        normed = (parts[j] * scale * gain_ref[pl.ds(r ^ j, 1), :]).astype(BF)
        gate = gate + jnp.dot(normed, wg_ref[at, :], preferred_element_type=F32)
        upper = upper + jnp.dot(normed, wu_ref[at, :], preferred_element_type=F32)
    active = (gate / (1.0 + jnp.exp(-gate)) * upper).astype(BF)
    for j in range(4):
        at = pl.ds(pl.multiple_of((r ^ j) * width, 128), width)
        terms = matmul_t(active, wd_ref[at, :]).astype(BF)
        if j == 0:
            o0[...] = terms
        elif j == 2:
            o2[...] = terms
        else:
            o13[j // 2] = terms


def ffn(r, gain, wg, wu, wd, parts):
    rows, width = parts[0].shape
    step = 256 if rows % 256 == 0 else 192
    whole = pl.BlockSpec(wg.shape, lambda i: (0, 0))
    tile = pl.BlockSpec((step, width), lambda i: (i, 0))
    return pl.pallas_call(
        ffn_kernel,
        grid=(rows // step,),
        out_shape=(
            jax.ShapeDtypeStruct((rows, width), BF),
            jax.ShapeDtypeStruct((2, rows, width), BF),
            jax.ShapeDtypeStruct((rows, width), BF),
        ),
        in_specs=[SMEM, pl.BlockSpec(gain.shape, lambda i: (0, 0)), whole, whole, whole] + [tile] * 4,
        out_specs=(tile, pl.BlockSpec((2, step, width), lambda i: (0, i, 0)), tile),
        compiler_params=PARAMS,
        name="ffn",
    )(r, gain, wg, wu, wd, *parts)


def local(
    queries,
    suffix_keys,
    suffix_values,
    prefix_keys,
    prefix_values,
    sink_logits,
    suffix_lengths,
    out_weight,
    residual,
    norm_gain,
    expert_ids,
    gate_fixed,
    gate_weight,
    up_weight,
    down_weight,
):
    tokens = queries.shape[0]
    ring = lax.axis_size("col")
    rows4 = lax.axis_size("row")
    z = lax.axis_index("col").astype(jnp.int32)
    z1 = z.reshape(1)
    r1 = lax.axis_index("row").astype(jnp.int32).reshape(1)
    ends = jnp.cumsum(suffix_lengths[0]).astype(jnp.int32)
    info = jnp.concatenate([ends, z1])

    def shift(x, k):
        return lax.ppermute(x, "col", [(i, (i + k) % ring) for i in range(ring)])

    def swap(x, k):
        return lax.ppermute(x, "row", [(i, i ^ k) for i in range(rows4)])

    def both_ways(own, low, high, work=None):
        found = {0: own}
        up, down = own, own
        for k in range(1, 4):
            up, down = shift(up, 1), shift(down, -1)
            if work is not None:
                up, down = work(k - 1, found, up, down)
            found[k], found[-k] = up, down
        found[4] = (shift(low(up), 1), shift(high(down), -1))
        return found

    half = prefix_keys.shape[1] + tokens
    kv = jnp.concatenate([prefix_keys[0], suffix_keys, prefix_values[0], suffix_values], axis=0)
    states = [None]

    def work(k, found, up, down):
        blocks = [found[k], found[-k]] if k else [found[0]]
        state = attend(
            info, sink_logits, queries, states[-1], blocks, (k, -k) if k else (0,), ring, False
        )
        up, down, state = lax.optimization_barrier((up, down, state))
        states.append(state)
        return up, down

    found = both_ways(kv, lambda x: x[:half], lambda x: x[half:], work)
    state = attend(
        info, sink_logits, queries, states[-1], [found[3], found[-3]], (3, -3), ring, False
    )
    gates = gate_fixed.T
    table = jnp.concatenate([expert_ids.T, gates // 64, gates % 64], axis=1).astype(BF)
    columns, features = out_weight.shape[1], out_weight.shape[0]
    table = jnp.pad(table, ((0, PAD - TOPK), (0, features - table.shape[1])))
    gathered = lax.all_gather(
        jnp.concatenate([out_weight.T, table], axis=0), "col", axis=0, tiled=True
    )
    stride = columns + PAD
    extras = gathered.reshape(ring, stride, features)[:, columns:, : 3 * tokens]

    attended = attend(info, sink_logits, queries, state, found[4], (4,), ring, True)
    own, across, pair = project(r1, attended, gathered, stride)
    pair = swap(pair, 1).astype(F32)
    across = swap((across + pair[1]).astype(BF), 2).astype(F32)
    hidden = (residual.astype(F32) + (own + pair[0] + across)).astype(BF)

    middle = tokens // 2
    order = (0, 1, -1, 2, -2, 3, -3, 4)
    size = len(order) // CHUNKS
    gain = norm_gain.reshape(rows4, -1)
    width = hidden.shape[1]
    chunks = [order[c * size : (c + 1) * size] for c in range(CHUNKS)]
    arrived = {}

    def dispatch(offsets, found):
        outgoing = select(z1, extras, [found[k] for k in offsets], offsets, ring)
        received = lax.all_to_all(outgoing, "grp", split_axis=0, concat_axis=0, tiled=True)
        arrived[offsets] = received.reshape(-1, width)

    def early(k, found, up, down):
        if k == 1:
            dispatch(chunks[0], {**found, 2: up, -2: down})
            up, down, arrived[chunks[0]] = lax.optimization_barrier(
                (up, down, arrived[chunks[0]])
            )
        return up, down

    found = both_ways(hidden, lambda x: x[:middle], lambda x: x[middle:], early)
    found[4] = jnp.concatenate(found[4], axis=0)
    sums = {}
    for offsets in chunks:
        if offsets not in arrived:
            dispatch(offsets, found)
        x0 = arrived[offsets]
        x2 = swap(x0, 2)
        x1 = swap(x0, 1)
        x3 = swap(x2, 1)
        o0, o13, o2 = ffn(r1, gain, gate_weight[0], up_weight[0], down_weight[0], (x0, x1, x2, x3))
        k13 = swap(o13, 1).astype(F32)
        far = swap((o2.astype(F32) + k13[1]).astype(BF), 2)
        result = (o0.astype(F32) + k13[0] + far.astype(F32)).astype(BF)
        returned = lax.all_to_all(
            result.reshape(8, -1, width), "grp", split_axis=0, concat_axis=0, tiled=True
        )
        mixed = combine(z1, extras, returned, offsets, ring, tokens)
        for i, k in enumerate(offsets):
            sums[k] = mixed[i]

    low = shift(sums[4][:middle].astype(BF), -1).astype(F32)
    high = shift(sums[4][middle:].astype(BF), 1).astype(F32)
    down = sums[3] + jnp.pad(low, ((0, middle), (0, 0)))
    up = sums[-3] + jnp.pad(high, ((middle, 0), (0, 0)))
    for k in (2, 1, 0):
        down, up = lax.optimization_barrier((down.astype(BF), up.astype(BF)))
        down, up = lax.optimization_barrier((shift(down, -1), shift(up, 1)))
        down, up = down.astype(F32), up.astype(F32)
        if k:
            down, up = sums[k] + down, sums[-k] + up
    expert_mix = (sums[0] + down + up).astype(BF)
    return (hidden, expert_mix)


def solution(mesh):
    placed = (
        P(("grp", "col"), "row"),
        P(("grp", "col"), "row"),
        P(("grp", "col"), "row"),
        P("grp", "col", "row"),
        P("grp", "col", "row"),
        P("row"),
        P("grp", None),
        P("row", "col"),
        P(("grp", "col"), "row"),
        P(),
        P(("grp", "col"), None),
        P(("grp", "col"), None),
        P(("grp", "col"), None, "row"),
        P(("grp", "col"), None, "row"),
        P(("grp", "col"), None, "row"),
    )
    return jax.shard_map(
        local,
        mesh=mesh,
        in_specs=placed,
        out_specs=(P(("grp", "col"), "row"), P(("grp", "col"), "row")),
        check_vma=False,
    )
```

```python
import functools

import jax
import jax.numpy as jnp
from jax import lax
from jax.experimental import pallas as pl
from jax.experimental.pallas import tpu as pltpu
from jax.sharding import PartitionSpec as P


HD = 128
TOPK = 6
CAP = 24
CHUNKS = 2
PAD = 16
eps = 1e-06
BF = jnp.bfloat16
F32 = jnp.float32
VMEM = pl.BlockSpec(memory_space=pltpu.VMEM)
SMEM = pl.BlockSpec(memory_space=pltpu.SMEM)
PARAMS = pltpu.CompilerParams(vmem_limit_bytes=56 * 1024 * 1024)


def matmul_t(a, b):
    return lax.dot_general(a, b, (((1,), (1,)), ((), ())), preferred_element_type=F32)


def pack_kernel(pk_ref, sk_ref, pv_ref, sv_ref, w_ref, ids_ref, gate_ref, out_ref):
    at = 0
    pieces = [pk_ref[0], sk_ref[...], pv_ref[0], sv_ref[...]]
    pieces += [w_ref[:, i * HD : (i + 1) * HD] for i in range(w_ref.shape[1] // HD)]
    gates = gate_ref[...]
    blank = jnp.zeros((PAD - TOPK, gates.shape[1]), BF)
    for x in (ids_ref[...], gates >> 6, gates & 63):
        pieces.append(jnp.concatenate([x.astype(F32), blank.astype(F32)], axis=0).astype(BF))
    for piece in pieces:
        out_ref[at : at + piece.shape[0]] = piece
        at += piece.shape[0]


def pack(*args):
    keys, fresh, turned = args[0], args[1], args[4]
    rows = 2 * (keys.shape[1] + fresh.shape[0]) + turned.size // HD + 3 * PAD
    return pl.pallas_call(
        pack_kernel,
        out_shape=jax.ShapeDtypeStruct((rows, HD), BF),
        in_specs=[VMEM] * len(args),
        out_specs=VMEM,
        compiler_params=PARAMS,
        name="pack",
    )(*args)


def attend_kernel(first, last, offsets, ring, half, info_ref, sink_ref, q_ref, *refs):
    blocks, refs = refs[: len(offsets)], refs[len(offsets) :]
    tokens = q_ref.shape[0]
    heads = q_ref.shape[1] // HD
    rows = tokens * heads
    q = jnp.concatenate([q_ref[:, h * HD : (h + 1) * HD] for h in range(heads)], axis=0)
    if first:
        top = jnp.concatenate(
            [jnp.full((tokens, 1), sink_ref[h], F32) for h in range(heads)], axis=0
        )
        total = jnp.ones((rows, 1), F32)
        acc = jnp.zeros((rows, HD), F32)
    else:
        top, total, acc = refs[0][:, :1], refs[1][:, :1], refs[2][...]
        refs = refs[3:]
    z = info_ref[4]
    token = lax.rem(lax.broadcasted_iota(jnp.int32, (rows, 1), 0), tokens)
    q_pos = z * tokens + token
    begin = jnp.zeros_like(q_pos)
    for i in range(4):
        end = info_ref[i]
        begin = jnp.maximum(begin, jnp.where(q_pos >= end, end, 0))
    for i, offset in enumerate(offsets):
        keys, values = blocks[i][:half], blocks[i][half : 2 * half]
        shared = keys.shape[0] - tokens
        scores = matmul_t(q, keys) * HD ** (-0.5)
        source = lax.rem(z - offset + ring, ring)
        k_pos = source * tokens + lax.broadcasted_iota(jnp.int32, (1, tokens), 1)
        visible = (k_pos >= begin) & (k_pos <= q_pos)
        scores = jnp.concatenate(
            [scores[:, :shared], jnp.where(visible, scores[:, shared:], -1e30)], axis=1
        )
        new_top = jnp.maximum(top, jnp.max(scores, axis=1, keepdims=True))
        weights = jnp.exp(scores - new_top)
        factor = jnp.exp(top - new_top)
        total = total * factor + jnp.sum(weights, axis=1, keepdims=True)
        acc = acc * factor + jnp.dot(weights.astype(BF), values, preferred_element_type=F32)
        top = new_top
    if last:
        out = (acc / total).astype(BF)
        for h in range(heads):
            refs[0][:, h * HD : (h + 1) * HD] = out[h * tokens : (h + 1) * tokens]
    else:
        refs[0][...] = jnp.broadcast_to(top, (rows, HD))
        refs[1][...] = jnp.broadcast_to(total, (rows, HD))
        refs[2][...] = acc


def attend(info, sinks, queries, state, blocks, offsets, ring, half, last):
    tokens = queries.shape[0]
    rows = tokens * (queries.shape[1] // HD)
    first = state is None
    state = () if first else tuple(state)
    if last:
        out_shape = jax.ShapeDtypeStruct(queries.shape, BF)
        out_specs = VMEM
    else:
        out_shape = (jax.ShapeDtypeStruct((rows, HD), F32),) * 3
        out_specs = (VMEM,) * 3
    return pl.pallas_call(
        functools.partial(attend_kernel, first, last, tuple(offsets), ring, half),
        out_shape=out_shape,
        in_specs=[SMEM, SMEM] + [VMEM] * (1 + len(blocks) + len(state)),
        out_specs=out_specs,
        compiler_params=PARAMS,
        name="attend",
    )(info, sinks, queries, *blocks, *state)


def project_kernel(order, ring, start, info_ref, a_ref, *refs):
    blocks, (own_ref, across_ref, pair_ref, ex_ref, parts) = refs[:-5], refs[-5:]
    tail = ex_ref.shape[1]
    z, r = info_ref[4], info_ref[5]
    width = parts.shape[3]
    a = a_ref[...]
    chunks = a.shape[1] // HD
    for k, block in zip(order, blocks):
        if k == 4:
            pieces = [block[start : start + width]]
            rest = blocks[-1]
            pieces += [rest[i * width : (i + 1) * width] for i in range(chunks - 1)]
        else:
            pieces = [block[start + i * width : start + (i + 1) * width] for i in range(chunks)]
        ex_ref[k % ring] = (blocks[-1] if k == 4 else block)[-tail:]
        part = matmul_t(a, jnp.concatenate(pieces, axis=1))
        source = lax.rem(z - k + ring, ring)
        parts[r ^ (source // 2), source % 2] = part
    for half in range(2):
        cols = slice(half * width, (half + 1) * width)
        own_ref[:, cols] = parts[0, half]
        across_ref[:, cols] = parts[2, half]
        pair_ref[0, :, cols] = parts[1, half].astype(BF)
        pair_ref[1, :, cols] = parts[3, half].astype(BF)


def project(info, attended, blocks, order, ring, start, width):
    tokens = attended.shape[0]
    return pl.pallas_call(
        functools.partial(project_kernel, order, ring, start),
        out_shape=(
            jax.ShapeDtypeStruct((tokens, 2 * width), F32),
            jax.ShapeDtypeStruct((tokens, 2 * width), F32),
            jax.ShapeDtypeStruct((2, tokens, 2 * width), BF),
            jax.ShapeDtypeStruct((ring, 3 * PAD, tokens), BF),
        ),
        in_specs=[SMEM] + [VMEM] * (1 + len(blocks)),
        out_specs=(VMEM,) * 4,
        scratch_shapes=[pltpu.VMEM((4, 2, tokens, width), F32)],
        compiler_params=PARAMS,
        name="project",
    )(info, attended, *blocks)


def routing(ids, z, ring):
    tokens = ids.shape[1]
    experts = (lax.broadcasted_iota(jnp.int32, (8, tokens), 0) * ring + z).astype(F32)
    hits = [(ids[k : k + 1] == experts).astype(F32) for k in range(TOPK)]
    chosen = sum(hits)
    before = (
        lax.broadcasted_iota(jnp.int32, (tokens, tokens), 0)
        < lax.broadcasted_iota(jnp.int32, (tokens, tokens), 1)
    ).astype(BF)
    slot = jnp.dot(chosen.astype(BF), before, preferred_element_type=F32)
    slot = jnp.where(chosen > 0, slot, -1.0)
    place = lax.broadcasted_iota(jnp.int32, (8, CAP, tokens), 1).astype(F32)
    picks = (place == slot[:, None, :]).astype(F32)
    return hits, picks


def select_kernel(offsets, ring, z_ref, ex_ref, *refs):
    z = z_ref[0]
    out_ref = refs[-1]
    for i, offset in enumerate(offsets):
        tokens = refs[i].shape[0]
        _, picks = routing(ex_ref[offset % ring, :TOPK].astype(F32), z, ring)
        picks = picks.reshape(8 * CAP, tokens).astype(BF)
        rows = jnp.dot(picks, refs[i][...], preferred_element_type=F32).astype(BF)
        for g in range(8):
            out_ref[g, i * CAP : (i + 1) * CAP, :] = rows[g * CAP : (g + 1) * CAP]


def select(z, extras, blocks, offsets, ring):
    width = blocks[0].shape[1]
    return pl.pallas_call(
        functools.partial(select_kernel, tuple(offsets), ring),
        out_shape=jax.ShapeDtypeStruct((8, CAP * len(blocks), width), BF),
        in_specs=[SMEM, VMEM] + [VMEM] * len(blocks),
        out_specs=VMEM,
        compiler_params=PARAMS,
        name="select",
    )(z, extras, *blocks)


def combine_kernel(offsets, ring, z_ref, ex_ref, ret_ref, out_ref):
    z = z_ref[0]
    tokens = out_ref.shape[1]
    for i, offset in enumerate(offsets):
        table = ex_ref[offset % ring].astype(F32)
        hits, picks = routing(table[:TOPK], z, ring)
        gates = 64.0 * table[PAD : PAD + TOPK] + table[2 * PAD : 2 * PAD + TOPK]
        shares = gates / jnp.sum(gates, axis=0, keepdims=True)
        mine = sum(hits[k] * shares[k : k + 1] for k in range(TOPK))
        weights = (picks * mine[:, None, :]).reshape(8 * CAP, tokens)
        high = weights.astype(BF)
        low = (weights - high.astype(F32)).astype(BF)
        rows = jnp.concatenate([ret_ref[g, i * CAP : (i + 1) * CAP, :] for g in range(8)], axis=0)
        dims = (((0,), (0,)), ((), ()))
        out_ref[i] = lax.dot_general(
            high, rows, dims, preferred_element_type=F32
        ) + lax.dot_general(low, rows, dims, preferred_element_type=F32)


def combine(z, extras, returned, offsets, ring, tokens):
    width = returned.shape[2]
    return pl.pallas_call(
        functools.partial(combine_kernel, tuple(offsets), ring),
        out_shape=jax.ShapeDtypeStruct((len(offsets), tokens, width), F32),
        in_specs=[SMEM, VMEM, VMEM],
        out_specs=VMEM,
        compiler_params=PARAMS,
        name="combine",
    )(z, extras, returned)


def ffn_kernel(r_ref, gain_ref, wg_ref, wu_ref, wd_ref, x0, x1, x2, x3, o0, o13, o2):
    r = r_ref[0]
    parts = [x[...].astype(F32) for x in (x0, x1, x2, x3)]
    width = parts[0].shape[1]
    square = sum(jnp.sum(p * p, axis=1, keepdims=True) for p in parts)
    scale = lax.rsqrt(square * (1.0 / (4 * width)) + eps)
    gate, upper = 0.0, 0.0
    for j in range(4):
        at = pl.ds(pl.multiple_of((r ^ j) * width, 128), width)
        normed = (parts[j] * scale * gain_ref[pl.ds(r ^ j, 1), :]).astype(BF)
        gate = gate + jnp.dot(normed, wg_ref[at, :], preferred_element_type=F32)
        upper = upper + jnp.dot(normed, wu_ref[at, :], preferred_element_type=F32)
    active = (gate / (1.0 + jnp.exp(-gate)) * upper).astype(BF)
    for j in range(4):
        at = pl.ds(pl.multiple_of((r ^ j) * width, 128), width)
        terms = matmul_t(active, wd_ref[at, :]).astype(BF)
        if j == 0:
            o0[...] = terms
        elif j == 2:
            o2[...] = terms
        else:
            o13[j // 2] = terms


def ffn(r, gain, wg, wu, wd, parts):
    rows, width = parts[0].shape
    step = 256 if rows % 256 == 0 else 192
    whole = pl.BlockSpec(wg.shape, lambda i: (0, 0))
    tile = pl.BlockSpec((step, width), lambda i: (i, 0))
    return pl.pallas_call(
        ffn_kernel,
        grid=(rows // step,),
        out_shape=(
            jax.ShapeDtypeStruct((rows, width), BF),
            jax.ShapeDtypeStruct((2, rows, width), BF),
            jax.ShapeDtypeStruct((rows, width), BF),
        ),
        in_specs=[SMEM, pl.BlockSpec(gain.shape, lambda i: (0, 0)), whole, whole, whole] + [tile] * 4,
        out_specs=(tile, pl.BlockSpec((2, step, width), lambda i: (0, i, 0)), tile),
        compiler_params=PARAMS,
        name="ffn",
    )(r, gain, wg, wu, wd, *parts)


def local(
    queries,
    suffix_keys,
    suffix_values,
    prefix_keys,
    prefix_values,
    sink_logits,
    suffix_lengths,
    out_weight,
    residual,
    norm_gain,
    expert_ids,
    gate_fixed,
    gate_weight,
    up_weight,
    down_weight,
):
    tokens = queries.shape[0]
    ring = lax.axis_size("col")
    rows4 = lax.axis_size("row")
    z = lax.axis_index("col").astype(jnp.int32)
    z1 = z.reshape(1)
    r1 = lax.axis_index("row").astype(jnp.int32).reshape(1)
    ends = jnp.cumsum(suffix_lengths[0]).astype(jnp.int32)
    info = jnp.concatenate([ends, z1, r1])

    def shift(x, k):
        return lax.ppermute(x, "col", [(i, (i + k) % ring) for i in range(ring)])

    def swap(x, k):
        return lax.ppermute(x, "row", [(i, i ^ k) for i in range(rows4)])

    def both_ways(own, low, high, work=None):
        found = {0: own}
        up, down = own, own
        for k in range(1, 4):
            up, down = shift(up, 1), shift(down, -1)
            if work is not None:
                up, down = work(k - 1, found, up, down)
            found[k], found[-k] = up, down
        found[4] = (shift(low(up), 1), shift(high(down), -1))
        return found

    half = prefix_keys.shape[1] + tokens
    columns = out_weight.shape[1]
    load = pack(
        prefix_keys,
        suffix_keys,
        prefix_values,
        suffix_values,
        out_weight.T,
        expert_ids.T,
        gate_fixed.T,
    )
    cut = 2 * half + columns
    states = [None]

    def work(k, found, up, down):
        blocks = [found[k], found[-k]] if k else [found[0]]
        state = attend(
            info, sink_logits, queries, states[-1], blocks, (k, -k) if k else (0,), ring, half, False
        )
        up, down, state = lax.optimization_barrier((up, down, state))
        states.append(state)
        return up, down

    found = both_ways(load, lambda x: x[:cut], lambda x: x[cut:], work)
    state = attend(
        info, sink_logits, queries, states[-1], [found[3], found[-3]], (3, -3), ring, half, False
    )
    attended = attend(
        info, sink_logits, queries, state, found[4][:1], (4,), ring, half, True
    )
    order = (0, 1, -1, 2, -2, 3, -3, 4)
    blocks = [found[k] for k in order[:-1]] + list(found[4])
    own, across, pair, extras = project(info, attended, blocks, order, ring, 2 * half, columns)
    pair = swap(pair, 1).astype(F32)
    across = swap((across + pair[1]).astype(BF), 2).astype(F32)
    hidden = (residual.astype(F32) + (own + pair[0] + across)).astype(BF)

    middle = tokens // 2
    size = len(order) // CHUNKS
    gain = norm_gain.reshape(rows4, -1)
    width = hidden.shape[1]
    chunks = [order[c * size : (c + 1) * size] for c in range(CHUNKS)]
    arrived = {}

    def dispatch(offsets, found):
        outgoing = select(z1, extras, [found[k] for k in offsets], offsets, ring)
        received = lax.all_to_all(outgoing, "grp", split_axis=0, concat_axis=0, tiled=True)
        arrived[offsets] = received.reshape(-1, width)

    def early(k, found, up, down):
        if k == 1:
            dispatch(chunks[0], {**found, 2: up, -2: down})
            up, down, arrived[chunks[0]] = lax.optimization_barrier(
                (up, down, arrived[chunks[0]])
            )
        return up, down

    found = both_ways(hidden, lambda x: x[:middle], lambda x: x[middle:], early)
    found[4] = jnp.concatenate(found[4], axis=0)
    sums = {}
    for offsets in chunks:
        if offsets not in arrived:
            dispatch(offsets, found)
        x0 = arrived[offsets]
        x2 = swap(x0, 2)
        x1 = swap(x0, 1)
        x3 = swap(x2, 1)
        o0, o13, o2 = ffn(r1, gain, gate_weight[0], up_weight[0], down_weight[0], (x0, x1, x2, x3))
        k13 = swap(o13, 1).astype(F32)
        far = (o2.astype(F32) + k13[1]).astype(BF)
        far = swap(far, 2)
        result = (o0.astype(F32) + k13[0] + far.astype(F32)).astype(BF)
        result = result.reshape(8, -1, width)
        returned = lax.all_to_all(result, "grp", split_axis=0, concat_axis=0, tiled=True)
        mixed = combine(z1, extras, returned, offsets, ring, tokens)
        for i, k in enumerate(offsets):
            sums[k] = mixed[i]

    low = shift(sums[4][:middle].astype(BF), -1).astype(F32)
    high = shift(sums[4][middle:].astype(BF), 1).astype(F32)
    down = sums[3] + jnp.pad(low, ((0, middle), (0, 0)))
    up = sums[-3] + jnp.pad(high, ((middle, 0), (0, 0)))
    for k in (2, 1, 0):
        down, up = lax.optimization_barrier((down.astype(BF), up.astype(BF)))
        down, up = lax.optimization_barrier((shift(down, -1), shift(up, 1)))
        down, up = down.astype(F32), up.astype(F32)
        if k:
            down, up = sums[k] + down, sums[-k] + up
    expert_mix = (sums[0] + down + up).astype(BF)
    return (hidden, expert_mix)


def solution(mesh):
    placed = (
        P(("grp", "col"), "row"),
        P(("grp", "col"), "row"),
        P(("grp", "col"), "row"),
        P("grp", "col", "row"),
        P("grp", "col", "row"),
        P("row"),
        P("grp", None),
        P("row", "col"),
        P(("grp", "col"), "row"),
        P(),
        P(("grp", "col"), None),
        P(("grp", "col"), None),
        P(("grp", "col"), None, "row"),
        P(("grp", "col"), None, "row"),
        P(("grp", "col"), None, "row"),
    )
    return jax.shard_map(
        local,
        mesh=mesh,
        in_specs=placed,
        out_specs=(P(("grp", "col"), "row"), P(("grp", "col"), "row")),
        check_vma=False,
    )
```

```python
import functools

import jax
import jax.numpy as jnp
from jax import lax
from jax.experimental import pallas as pl
from jax.experimental.pallas import tpu as pltpu
from jax.sharding import PartitionSpec as P


HD = 128
TOPK = 6
CAP = 24
PAD = 16
eps = 1e-06
BF = jnp.bfloat16
F32 = jnp.float32
VMEM = pl.BlockSpec(memory_space=pltpu.VMEM)
SMEM = pl.BlockSpec(memory_space=pltpu.SMEM)
PARAMS = pltpu.CompilerParams(vmem_limit_bytes=56 * 1024 * 1024)


def matmul_t(a, b):
    return lax.dot_general(a, b, (((1,), (1,)), ((), ())), preferred_element_type=F32)


def pack_kernel(pk_ref, sk_ref, pv_ref, sv_ref, w_ref, ids_ref, gate_ref, out_ref):
    at = 0
    pieces = [pk_ref[0], sk_ref[...], pv_ref[0], sv_ref[...]]
    pieces += [w_ref[:, i * HD : (i + 1) * HD] for i in range(w_ref.shape[1] // HD)]
    gates = gate_ref[...]
    blank = jnp.zeros((PAD - TOPK, gates.shape[1]), BF)
    for x in (ids_ref[...], gates >> 6, gates & 63):
        pieces.append(jnp.concatenate([x.astype(F32), blank.astype(F32)], axis=0).astype(BF))
    for piece in pieces:
        out_ref[at : at + piece.shape[0]] = piece
        at += piece.shape[0]


def pack(*args):
    keys, fresh, turned = args[0], args[1], args[4]
    rows = 2 * (keys.shape[1] + fresh.shape[0]) + turned.size // HD + 3 * PAD
    return pl.pallas_call(
        pack_kernel,
        out_shape=jax.ShapeDtypeStruct((rows, HD), BF),
        in_specs=[VMEM] * len(args),
        out_specs=VMEM,
        compiler_params=PARAMS,
        name="pack",
    )(*args)


def attend_kernel(first, last, offsets, ring, half, info_ref, sink_ref, q_ref, *refs):
    blocks, refs = refs[: len(offsets)], refs[len(offsets) :]
    tokens = q_ref.shape[0]
    heads = q_ref.shape[1] // HD
    z = info_ref[4]
    q_pos = z * tokens + lax.broadcasted_iota(jnp.int32, (tokens, 1), 0)
    begin = jnp.zeros_like(q_pos)
    for i in range(4):
        end = info_ref[i]
        begin = jnp.maximum(begin, jnp.where(q_pos >= end, end, 0))
    seen = []
    for offset in offsets:
        source = lax.rem(z - offset + ring, ring)
        k_pos = source * tokens + lax.broadcasted_iota(jnp.int32, (1, tokens), 1)
        seen.append((k_pos >= begin) & (k_pos <= q_pos))

    def head(h, carry):
        lanes = pl.ds(pl.multiple_of(h * HD, HD), HD)
        band = pl.ds(pl.multiple_of(h * tokens, HD), tokens)
        q = q_ref[:, lanes]
        if first:
            top = jnp.full((tokens, 1), sink_ref[h], F32)
            total = jnp.ones((tokens, 1), F32)
            acc = jnp.zeros((tokens, HD), F32)
        else:
            top, total, acc = refs[0][band, :1], refs[1][band, :1], refs[2][band]
        for block, visible in zip(blocks, seen):
            scores = matmul_t(q, block[:half]) * HD ** (-0.5)
            shared = half - tokens
            scores = jnp.concatenate(
                [scores[:, :shared], jnp.where(visible, scores[:, shared:], -1e30)], axis=1
            )
            new_top = jnp.maximum(top, jnp.max(scores, axis=1, keepdims=True))
            weights = jnp.exp(scores - new_top)
            factor = jnp.exp(top - new_top)
            total = total * factor + jnp.sum(weights, axis=1, keepdims=True)
            acc = acc * factor + jnp.dot(
                weights.astype(BF), block[half : 2 * half], preferred_element_type=F32
            )
            top = new_top
        if last:
            refs[-1][:, lanes] = (acc / total).astype(BF)
        else:
            refs[-3][band] = jnp.broadcast_to(top, (tokens, HD))
            refs[-2][band] = jnp.broadcast_to(total, (tokens, HD))
            refs[-1][band] = acc
        return carry

    if last:
        for h in range(heads):
            head(h, 0)
    else:
        lax.fori_loop(0, heads, head, 0)


def attend(info, sinks, queries, state, blocks, offsets, ring, half, last):
    tokens = queries.shape[0]
    rows = tokens * (queries.shape[1] // HD)
    first = state is None
    state = () if first else tuple(state)
    if last:
        out_shape = jax.ShapeDtypeStruct(queries.shape, BF)
        out_specs = VMEM
    else:
        out_shape = (jax.ShapeDtypeStruct((rows, HD), F32),) * 3
        out_specs = (VMEM,) * 3
    return pl.pallas_call(
        functools.partial(attend_kernel, first, last, tuple(offsets), ring, half),
        out_shape=out_shape,
        in_specs=[SMEM, SMEM] + [VMEM] * (1 + len(blocks) + len(state)),
        out_specs=out_specs,
        compiler_params=PARAMS,
        name="attend",
    )(info, sinks, queries, *blocks, *state)


def project_kernel(order, ring, start, info_ref, a_ref, *refs):
    blocks, (own_ref, across_ref, pair_ref, ex_ref, parts) = refs[:-5], refs[-5:]
    tail = ex_ref.shape[1]
    z, r = info_ref[4], info_ref[5]
    width = parts.shape[3]
    a = a_ref[...]
    chunks = a.shape[1] // HD
    for k, block in zip(order, blocks):
        if k == 4:
            pieces = [block[start : start + width]]
            rest = blocks[-1]
            pieces += [rest[i * width : (i + 1) * width] for i in range(chunks - 1)]
        else:
            pieces = [block[start + i * width : start + (i + 1) * width] for i in range(chunks)]
        ex_ref[k % ring] = (blocks[-1] if k == 4 else block)[-tail:]
        part = matmul_t(a, jnp.concatenate(pieces, axis=1))
        source = lax.rem(z - k + ring, ring)
        parts[r ^ (source // 2), source % 2] = part
    for half in range(2):
        cols = slice(half * width, (half + 1) * width)
        own_ref[:, cols] = parts[0, half]
        across_ref[:, cols] = parts[2, half]
        pair_ref[0, :, cols] = parts[1, half].astype(BF)
        pair_ref[1, :, cols] = parts[3, half].astype(BF)


def project(info, attended, blocks, order, ring, start, width):
    tokens = attended.shape[0]
    return pl.pallas_call(
        functools.partial(project_kernel, order, ring, start),
        out_shape=(
            jax.ShapeDtypeStruct((tokens, 2 * width), F32),
            jax.ShapeDtypeStruct((tokens, 2 * width), F32),
            jax.ShapeDtypeStruct((2, tokens, 2 * width), BF),
            jax.ShapeDtypeStruct((ring, 3 * PAD, tokens), BF),
        ),
        in_specs=[SMEM] + [VMEM] * (1 + len(blocks)),
        out_specs=(VMEM,) * 4,
        scratch_shapes=[pltpu.VMEM((4, 2, tokens, width), F32)],
        compiler_params=PARAMS,
        name="project",
    )(info, attended, *blocks)


def routing(ids, z, ring):
    tokens = ids.shape[1]
    experts = (lax.broadcasted_iota(jnp.int32, (8, tokens), 0) * ring + z).astype(F32)
    hits = [(ids[k : k + 1] == experts).astype(F32) for k in range(TOPK)]
    chosen = sum(hits)
    before = (
        lax.broadcasted_iota(jnp.int32, (tokens, tokens), 0)
        < lax.broadcasted_iota(jnp.int32, (tokens, tokens), 1)
    ).astype(BF)
    slot = jnp.dot(chosen.astype(BF), before, preferred_element_type=F32)
    slot = jnp.where(chosen > 0, slot, -1.0)
    place = lax.broadcasted_iota(jnp.int32, (8, CAP, tokens), 1).astype(F32)
    picks = (place == slot[:, None, :]).astype(F32)
    return hits, picks


def select_kernel(offsets, ring, z_ref, ex_ref, *refs):
    z = z_ref[0]
    out_ref = refs[-1]
    for i, offset in enumerate(offsets):
        tokens = refs[i].shape[0]
        _, picks = routing(ex_ref[offset % ring, :TOPK].astype(F32), z, ring)
        picks = picks.reshape(8 * CAP, tokens).astype(BF)
        rows = jnp.dot(picks, refs[i][...], preferred_element_type=F32).astype(BF)
        for g in range(8):
            out_ref[g, i * CAP : (i + 1) * CAP, :] = rows[g * CAP : (g + 1) * CAP]


def select(z, extras, blocks, offsets, ring):
    width = blocks[0].shape[1]
    return pl.pallas_call(
        functools.partial(select_kernel, tuple(offsets), ring),
        out_shape=jax.ShapeDtypeStruct((8, CAP * len(blocks), width), BF),
        in_specs=[SMEM, VMEM] + [VMEM] * len(blocks),
        out_specs=VMEM,
        compiler_params=PARAMS,
        name="select",
    )(z, extras, *blocks)


def combine_kernel(offsets, ring, z_ref, ex_ref, ret_ref, out_ref):
    z = z_ref[0]
    tokens = out_ref.shape[1]
    for i, offset in enumerate(offsets):
        table = ex_ref[offset % ring].astype(F32)
        hits, picks = routing(table[:TOPK], z, ring)
        gates = 64.0 * table[PAD : PAD + TOPK] + table[2 * PAD : 2 * PAD + TOPK]
        shares = gates / jnp.sum(gates, axis=0, keepdims=True)
        mine = sum(hits[k] * shares[k : k + 1] for k in range(TOPK))
        weights = (picks * mine[:, None, :]).reshape(8 * CAP, tokens)
        high = weights.astype(BF)
        low = (weights - high.astype(F32)).astype(BF)
        rows = jnp.concatenate([ret_ref[g, i * CAP : (i + 1) * CAP, :] for g in range(8)], axis=0)
        dims = (((0,), (0,)), ((), ()))
        out_ref[i] = lax.dot_general(
            high, rows, dims, preferred_element_type=F32
        ) + lax.dot_general(low, rows, dims, preferred_element_type=F32)


def combine(z, extras, returned, offsets, ring, tokens):
    width = returned.shape[2]
    return pl.pallas_call(
        functools.partial(combine_kernel, tuple(offsets), ring),
        out_shape=jax.ShapeDtypeStruct((len(offsets), tokens, width), F32),
        in_specs=[SMEM, VMEM, VMEM],
        out_specs=VMEM,
        compiler_params=PARAMS,
        name="combine",
    )(z, extras, returned)


def ffn_kernel(r_ref, gain_ref, wg_ref, wu_ref, wd_ref, x0, x1, x2, x3, o0, o13, o2):
    r = r_ref[0]
    parts = [x[...].astype(F32) for x in (x0, x1, x2, x3)]
    width = parts[0].shape[1]
    square = sum(jnp.sum(p * p, axis=1, keepdims=True) for p in parts)
    scale = lax.rsqrt(square * (1.0 / (4 * width)) + eps)
    gate, upper = 0.0, 0.0
    for j in range(4):
        at = pl.ds(pl.multiple_of((r ^ j) * width, 128), width)
        normed = (parts[j] * scale * gain_ref[pl.ds(r ^ j, 1), :]).astype(BF)
        gate = gate + jnp.dot(normed, wg_ref[at, :], preferred_element_type=F32)
        upper = upper + jnp.dot(normed, wu_ref[at, :], preferred_element_type=F32)
    active = (gate / (1.0 + jnp.exp(-gate)) * upper).astype(BF)
    for j in range(4):
        at = pl.ds(pl.multiple_of((r ^ j) * width, 128), width)
        terms = matmul_t(active, wd_ref[at, :]).astype(BF)
        if j == 0:
            o0[...] = terms
        elif j == 2:
            o2[...] = terms
        else:
            o13[j // 2] = terms


def ffn(r, gain, wg, wu, wd, parts):
    rows, width = parts[0].shape
    step = max(t for t in range(16, 336, 16) if rows % t == 0)
    whole = pl.BlockSpec(wg.shape, lambda i: (0, 0))
    tile = pl.BlockSpec((step, width), lambda i: (i, 0))
    return pl.pallas_call(
        ffn_kernel,
        grid=(rows // step,),
        out_shape=(
            jax.ShapeDtypeStruct((rows, width), BF),
            jax.ShapeDtypeStruct((2, rows, width), BF),
            jax.ShapeDtypeStruct((rows, width), BF),
        ),
        in_specs=[SMEM, pl.BlockSpec(gain.shape, lambda i: (0, 0)), whole, whole, whole] + [tile] * 4,
        out_specs=(tile, pl.BlockSpec((2, step, width), lambda i: (0, i, 0)), tile),
        compiler_params=PARAMS,
        name="ffn",
    )(r, gain, wg, wu, wd, *parts)


def local(
    queries,
    suffix_keys,
    suffix_values,
    prefix_keys,
    prefix_values,
    sink_logits,
    suffix_lengths,
    out_weight,
    residual,
    norm_gain,
    expert_ids,
    gate_fixed,
    gate_weight,
    up_weight,
    down_weight,
):
    tokens = queries.shape[0]
    ring = lax.axis_size("col")
    rows4 = lax.axis_size("row")
    z = lax.axis_index("col").astype(jnp.int32)
    z1 = z.reshape(1)
    r1 = lax.axis_index("row").astype(jnp.int32).reshape(1)
    ends = jnp.cumsum(suffix_lengths[0]).astype(jnp.int32)
    info = jnp.concatenate([ends, z1, r1])

    def shift(x, k):
        return lax.ppermute(x, "col", [(i, (i + k) % ring) for i in range(ring)])

    def swap(x, k):
        return lax.ppermute(x, "row", [(i, i ^ k) for i in range(rows4)])

    def both_ways(own, low, high, work=None):
        found = {0: own}
        up, down = own, own
        for k in range(1, 4):
            up, down = shift(up, 1), shift(down, -1)
            if work is not None:
                up, down = work(k - 1, found, up, down)
            found[k], found[-k] = up, down
        found[4] = (shift(low(up), 1), shift(high(down), -1))
        return found

    half = prefix_keys.shape[1] + tokens
    columns = out_weight.shape[1]
    load = pack(
        prefix_keys,
        suffix_keys,
        prefix_values,
        suffix_values,
        out_weight.T,
        expert_ids.T,
        gate_fixed.T,
    )
    cut = 2 * half + columns
    states = [None]

    def work(k, found, up, down):
        blocks = [found[k], found[-k]] if k else [found[0]]
        state = attend(
            info, sink_logits, queries, states[-1], blocks, (k, -k) if k else (0,), ring, half, False
        )
        up, down, state = lax.optimization_barrier((up, down, state))
        states.append(state)
        return up, down

    found = both_ways(load, lambda x: x[:cut], lambda x: x[cut:], work)
    state = attend(
        info, sink_logits, queries, states[-1], [found[3], found[-3]], (3, -3), ring, half, False
    )
    attended = attend(
        info, sink_logits, queries, state, found[4][:1], (4,), ring, half, True
    )
    order = (0, 1, -1, 2, -2, 3, -3, 4)
    blocks = [found[k] for k in order[:-1]] + list(found[4])
    own, across, pair, extras = project(info, attended, blocks, order, ring, 2 * half, columns)
    pair = swap(pair, 1).astype(F32)
    across = swap((across + pair[1]).astype(BF), 2).astype(F32)
    hidden = (residual.astype(F32) + (own + pair[0] + across)).astype(BF)

    middle = tokens // 2
    gain = norm_gain.reshape(rows4, -1)
    width = hidden.shape[1]
    chunks = [(4, 3, -3, 2, -2), (1, -1, 0)]
    arrived = {}

    def dispatch(offsets, found):
        outgoing = select(z1, extras, [found[k] for k in offsets], offsets, ring)
        received = lax.all_to_all(outgoing, "grp", split_axis=0, concat_axis=0, tiled=True)
        arrived[offsets] = received.reshape(-1, width)

    found = both_ways(hidden, lambda x: x[:middle], lambda x: x[middle:])
    found[4] = jnp.concatenate(found[4], axis=0)
    sums = {}
    for offsets in chunks:
        if offsets not in arrived:
            dispatch(offsets, found)
        x0 = arrived[offsets]
        x2 = swap(x0, 2)
        x1 = swap(x0, 1)
        x3 = swap(x2, 1)
        o0, o13, o2 = ffn(r1, gain, gate_weight[0], up_weight[0], down_weight[0], (x0, x1, x2, x3))
        k13 = swap(o13, 1).astype(F32)
        far = (o2.astype(F32) + k13[1]).astype(BF)
        far = swap(far, 2)
        result = (o0.astype(F32) + k13[0] + far.astype(F32)).astype(BF)
        result = result.reshape(8, -1, width)
        returned = lax.all_to_all(result, "grp", split_axis=0, concat_axis=0, tiled=True)
        mixed = combine(z1, extras, returned, offsets, ring, tokens)
        for i, k in enumerate(offsets):
            sums[k] = mixed[i]

    low = shift(sums[4][:middle].astype(BF), -1).astype(F32)
    high = shift(sums[4][middle:].astype(BF), 1).astype(F32)
    down = sums[3] + jnp.pad(low, ((0, middle), (0, 0)))
    up = sums[-3] + jnp.pad(high, ((middle, 0), (0, 0)))
    for k in (2, 1, 0):
        down, up = lax.optimization_barrier((down.astype(BF), up.astype(BF)))
        down, up = shift(down, -1), shift(up, 1)
        down, up = lax.optimization_barrier((down, up))
        down, up = down.astype(F32), up.astype(F32)
        if k:
            down, up = sums[k] + down, sums[-k] + up
    expert_mix = (sums[0] + down + up).astype(BF)
    return (hidden, expert_mix)


def solution(mesh):
    placed = (
        P(("grp", "col"), "row"),
        P(("grp", "col"), "row"),
        P(("grp", "col"), "row"),
        P("grp", "col", "row"),
        P("grp", "col", "row"),
        P("row"),
        P("grp", None),
        P("row", "col"),
        P(("grp", "col"), "row"),
        P(),
        P(("grp", "col"), None),
        P(("grp", "col"), None),
        P(("grp", "col"), None, "row"),
        P(("grp", "col"), None, "row"),
        P(("grp", "col"), None, "row"),
    )
    return jax.shard_map(
        local,
        mesh=mesh,
        in_specs=placed,
        out_specs=(P(("grp", "col"), "row"), P(("grp", "col"), "row")),
        check_vma=False,
    )
```
